32 devices in a mesh: row: 8 (over z, y), col: 4 (over x, core).
Axes of the slice: x: 2, y: 2, z: 4, core: 2. Of those that a mesh axis runs over, the one named last changes fastest.
Arguments:
- amplitudes: float32 [1024, 128, 128], P(('row', 'col')), may hold values from -6 to 6
- amp_owner: int32 [1024, 1], P(('row', 'col')), may hold values from 0 to 31; in each aligned block of 32 rows (0 to 31, 32 to 63, ...) at most 2 rows name the same one
- amp_occ: int32 [1024], P(('row', 'col')), may hold values from 0 to 11
- amp_vir: int32 [1024], P(('row', 'col')), may hold values from 0 to 31
- integrals: float32 [16384, 4, 128], P('col'), may hold values from -0.15625 to 0.15625
Outputs:
- residual: float32 [4, 12288, 128], P('col', 'row')
The draws below stay inside these ranges and needn't reach their ends.
Inputs may be any that keep to these rules, and one draw needn't show every extreme that they name: `amp_owner`: among the tiles listed on one device no owner is named more than 2 times, a bound that some block reaches.
All inputs are finite; a program needn't handle non-finite values.
Results may differ from the reference program's by a relative error of at most 0.0003.
Values sent between devices are 32-bit elements; how exact they have to be, the bound alone decides.
No kernel may reach another device: no remote copies, remote signals or barrier semaphores. Data moves between devices by JAX's collectives and lax.ppermute only.
A program may use at most 192 MiB of HBM per device.

```python
import math
import jax
import jax.numpy as jnp
import numpy as np
from jax import lax

TILE = 128
CAP = 2
OCC_DEV = 12
CV_DEV = 32
AMP_DEV = 32
NP = 96
NC = 128
NA_H = 4
N_ROW = 8
N_COL = 4
DEVICES = 32


def place_ends(drawn, own_key, least, high):
    shape = drawn.shape
    index_at = [jax.random.randint(jax.random.fold_in(own_key, axis), (), 0, shape[axis]) for axis in range(len(shape))]
    drawn = drawn.at[tuple(index_at)].set(least)
    longest = shape.index(max(shape))
    index_at[longest] = (index_at[longest] + 1) % shape[longest]
    return drawn.at[tuple(index_at)].set(high)


def block_scale(rng, dims, pieces, low, high):
    factor_of = 1.0
    for axis_at, shards_of in pieces:
        draws = jax.random.uniform(jax.random.fold_in(jax.random.fold_in(rng, 6), axis_at), (shards_of,), jnp.float32, low / len(pieces), high / len(pieces))
        factor_of = factor_of * jnp.repeat(jnp.exp(draws), dims[axis_at] // shards_of).reshape((-1,) + (1,) * (len(dims) - 1 - axis_at))
    return factor_of


def shared_out(stream_key, own, number, rows, amount, top, reach, skew):
    ranking = jax.random.permutation(stream_key, amount)
    crowded, usual = load_shares(amount, rows * top, reach, skew, True), load_shares(amount, rows * top, reach, skew, False)
    places = jnp.arange(amount)

    def named(tallies, rotation):
        used = int((tallies > 0).sum())
        fixed = max(1, used // 4)
        moved = fixed + (places - fixed + rotation * (used - fixed)) % max(1, amount - fixed)
        return jnp.zeros((amount,), jnp.int32).at[ranking[jnp.where(places < fixed, places, moved)]].set(jnp.asarray(tallies, jnp.int32))

    tallies = jnp.where(number % 4 == 0, named(crowded, number // 4), named(usual, number - number // 4 - 1))
    mixed = jax.random.permutation(jax.random.fold_in(own, 3), amount)
    donor, taker = mixed[0:amount // 2 * 2:2], mixed[1:amount // 2 * 2:2]
    slack = jnp.minimum(tallies[donor] - 1, reach - tallies[taker]) // 2
    slack = jnp.where((donor == ranking[0]) | (taker == ranking[0]) | (tallies[taker] == 0), 0, jnp.maximum(slack, 0))
    moved = jax.random.randint(jax.random.fold_in(own, 4), (amount // 2,), 0, 1 << 20) % (slack + 1)
    tallies = tallies.at[donor].add(-moved).at[taker].add(moved)
    labels = jnp.searchsorted(jnp.cumsum(tallies), jnp.arange(rows * top), side="right").astype(jnp.int32)
    listing = labels.reshape(top, rows).T
    listing = listing[jax.random.permutation(jax.random.fold_in(own, 1), rows)]
    rotation = jax.random.randint(jax.random.fold_in(own, 2), (rows, 1), 0, top)
    return jnp.take_along_axis(listing, (jnp.arange(top)[None, :] + rotation) % top, axis=1)


def load_shares(amount, total, most, skew, full):
    loads = [(1 << 20) // math.isqrt(grade ** skew) + 1 for grade in range(1, amount + 1)]
    largest = most if full else min(most, max(-(-total // amount), total * loads[0] // sum(loads)))
    least = 1 if total - largest >= amount - 1 else 0
    given, spare = [largest] + [least] * (amount - 1), total - largest - least * (amount - 1)
    while spare > 0:
        movable = [i for i in range(1, amount) if given[i] < largest] or [i for i in range(1, amount) if given[i] < most]
        pool, remaining = sum([loads[i] for i in movable]), spare
        for i in movable:
            more = min(most - given[i], max(1, remaining * loads[i] // pool), spare)
            given[i] = given[i] + more
            spare = spare - more
    return np.array(given)


def normal_values(own_key, shape, spread, limit, shards=(), kind=jnp.bfloat16):
    loudness = block_scale(own_key, shape, shards, -0.22, 0.18) if shards else 1.0
    drawn = jax.random.normal(own_key, shape, jnp.float32) * spread * loudness
    return jnp.minimum(jnp.maximum(drawn, -limit), limit).astype(kind)


def setup_inputs(seed: int = 0) -> dict:
    arg_keys = jax.random.split(jax.random.key(seed), 6)
    amplitudes = normal_values(arg_keys[0], (DEVICES * AMP_DEV, TILE, TILE), 1.0, 6.0, ((0, 32),), jnp.float32)
    amp_owner_keys = jax.random.split(jax.random.fold_in(arg_keys[1], 1), (DEVICES * AMP_DEV) // AMP_DEV)
    amp_owner_turns = jax.random.permutation(jax.random.fold_in(arg_keys[1], 3), (DEVICES * AMP_DEV) // AMP_DEV)
    amp_owner = jax.vmap(lambda own, number: shared_out(jax.random.fold_in(arg_keys[1], 2), own, number, AMP_DEV, DEVICES, 1, CAP, 2))(amp_owner_keys, amp_owner_turns).reshape((DEVICES * AMP_DEV, 1))
    amp_occ = place_ends(jax.random.randint(arg_keys[2], (DEVICES * AMP_DEV,), 0, OCC_DEV), jax.random.fold_in(arg_keys[2], 1), 0, OCC_DEV - 1).astype(jnp.int32)
    amp_vir = place_ends(jax.random.randint(arg_keys[3], (DEVICES * AMP_DEV,), 0, CV_DEV), jax.random.fold_in(arg_keys[3], 1), 0, CV_DEV - 1).astype(jnp.int32)
    integrals = normal_values(arg_keys[4], (NC * TILE, NA_H, TILE), (N_COL * AMP_DEV * TILE // OCC_DEV) ** -0.5, 0.15625, ((0, 4),), jnp.float32)
    return {"amplitudes": amplitudes, "amp_owner": amp_owner, "amp_occ": amp_occ, "amp_vir": amp_vir, "integrals": integrals}


def reference(amplitudes, amp_owner, amp_occ, amp_vir, integrals):
    owner = amp_owner[:, 0]
    row_of = owner // N_COL
    col_of = owner % N_COL
    vir_tile = col_of * CV_DEV + amp_vir
    blocks = integrals.reshape(NC, TILE, NA_H, TILE)
    dump = OCC_DEV * NC

    def one_row(which):
        target = jnp.where(row_of == which, amp_occ * NC + vir_tile, dump).astype(jnp.int32)
        grid = jnp.zeros((dump + 1, TILE, TILE), jnp.float32).at[target].add(amplitudes)
        grid = grid[:dump].reshape(OCC_DEV, NC, TILE, TILE)
        result = jnp.einsum('pcij,cjak->apik', grid, blocks, precision=lax.Precision.HIGHEST)
        return result.reshape(NA_H, OCC_DEV * TILE, TILE)

    stacked = lax.map(one_row, jnp.arange(N_ROW, dtype=jnp.int32))
    return jnp.transpose(stacked, (1, 0, 2, 3)).reshape(NA_H, NP * TILE, TILE)
```

```python
import functools

import jax
import jax.numpy as jnp
from jax import lax
from jax.experimental import pallas as pl
from jax.experimental.pallas import tpu as pltpu
from jax.sharding import PartitionSpec as P

CAP = 2
OCC_DEV = 12
CV_DEV = 32
NZ = 4
HEAD = 8
GROUPS = 2
SHIFT = 9
MASK = (1 << SHIFT) - 1
NBUF = 4
AXES = ("row", "col")
ANY = pl.BlockSpec(memory_space=pl.ANY)
f32 = jnp.float32
bf16 = jnp.bfloat16


def pack_kernel(tiles, devices, per_round, rnd, owner, occ, vir, amp, send, pay, held, count, index, head, sem_in, sem_a, sem_b, sem_h):
    edge = amp.shape[1]
    load = pltpu.make_async_copy(amp, held, sem_in)
    load.start()

    def clear(d, c):
        count[d] = 0
        index[CAP * d] = 0
        index[CAP * d + 1] = 0
        return c

    lax.fori_loop(0, devices, clear, 0)

    def place(t, c):
        o = owner[t]
        n = count[o]
        index[CAP * o + n] = t
        count[o] = n + 1
        return c

    lax.fori_loop(0, tiles, place, 0)
    base = rnd[0] * per_round

    def first(d):
        return pltpu.make_async_copy(held.at[index[CAP * d]], send.at[d], sem_a.at[d])

    def second(d, j):
        return pltpu.make_async_copy(held.at[index[CAP * d + 1]], pay.at[pl.ds(pl.multiple_of(j * edge, edge), edge), :], sem_b.at[j])

    def each(issue):
        def go(d, j):
            n = count[d]
            here = j - base
            inside = (n == 2) & (here >= 0) & (here < per_round)

            @pl.when(n >= 1)
            def _():
                first(d).start() if issue else first(d).wait()

            @pl.when(inside)
            def _():
                second(d, here).start() if issue else second(d, here).wait()

            if issue:
                t, u = index[CAP * d], index[CAP * d + 1]
                p = jnp.where(n >= 1, occ[t] * CV_DEV + vir[t] + 1, 0)
                q = jnp.where(n == 2, occ[u] * CV_DEV + vir[u] + 1, 0)
                head[0, d] = (p + (q << SHIFT) + (j << (2 * SHIFT))).astype(f32)
            return j + (n == 2).astype(jnp.int32)

        lax.fori_loop(0, devices, go, jnp.int32(0))

    load.wait()
    each(True)
    copy = pltpu.make_async_copy(head, pay.at[pl.ds(per_round * edge, HEAD), :], sem_h)
    copy.start()
    each(False)
    copy.wait()


def pack(rnd, owner, occ, vir, amp, devices, per_round):
    tiles, edge = amp.shape[:2]
    return pl.pallas_call(
        functools.partial(pack_kernel, tiles, devices, per_round),
        grid_spec=pltpu.PrefetchScalarGridSpec(
            num_scalar_prefetch=4,
            in_specs=[ANY],
            out_specs=[ANY, ANY],
            scratch_shapes=[
                pltpu.VMEM((tiles, edge, edge), f32),
                pltpu.SMEM((devices,), jnp.int32),
                pltpu.SMEM((CAP * devices,), jnp.int32),
                pltpu.SMEM((HEAD, 128), f32),
                pltpu.SemaphoreType.DMA,
                pltpu.SemaphoreType.DMA((devices,)),
                pltpu.SemaphoreType.DMA((per_round,)),
                pltpu.SemaphoreType.DMA,
            ],
        ),
        out_shape=[
            jax.ShapeDtypeStruct((devices, edge, edge), f32),
            jax.ShapeDtypeStruct((per_round * edge + HEAD, edge), f32),
        ],
        compiler_params=pltpu.CompilerParams(vmem_limit_bytes=40 << 20),
        name="pack",
    )(rnd, owner, occ, vir, amp)


def pick_kernel(layer, per_round, rnd, place, codes, *refs):
    line = refs[:NZ]
    outs = refs[NZ : NZ + layer]
    held, sem, sem_in, sem_out = refs[NZ + layer :]
    edge = line[0].shape[1]
    z, mine = place[0], place[1]
    loads = [pltpu.make_async_copy(line[k], held.at[k], sem_in.at[k]) for k in range(NZ)]
    for load in loads:
        load.start()
    for load in loads:
        load.wait()

    def moves(issue):
        for k in range(NZ):
            at = z ^ k
            for m in range(layer):
                code = codes[k, z * layer + (mine ^ m)]
                here = (code >> (2 * SHIFT)) - rnd[0] * per_round
                full = ((code >> SHIFT) & MASK) > 0

                @pl.when(full & (here >= 0) & (here < per_round))
                def _():
                    copy = pltpu.make_async_copy(
                        held.at[k, pl.ds(pl.multiple_of(here * edge, edge), edge), :],
                        outs[m].at[pl.ds(pl.multiple_of(at * edge, edge), edge), :],
                        sem.at[k, m],
                    )
                    copy.start() if issue else copy.wait()

                copy = pltpu.make_async_copy(
                    held.at[k, pl.ds(per_round * edge, HEAD), :],
                    outs[m].at[pl.ds(pl.multiple_of(NZ * edge + at * HEAD, HEAD), HEAD), :],
                    sem_out.at[k, m],
                )
                copy.start() if issue else copy.wait()

    moves(True)
    moves(False)


def pick(rnd, place, codes, arrays, layer, per_round):
    rows, edge = arrays[0].shape
    return pl.pallas_call(
        functools.partial(pick_kernel, layer, per_round),
        grid_spec=pltpu.PrefetchScalarGridSpec(
            num_scalar_prefetch=3,
            in_specs=[ANY] * NZ,
            out_specs=[ANY] * layer,
            scratch_shapes=[
                pltpu.VMEM((NZ, rows, edge), f32),
                pltpu.SemaphoreType.DMA((NZ, layer)),
                pltpu.SemaphoreType.DMA((NZ,)),
                pltpu.SemaphoreType.DMA((NZ, layer)),
            ],
        ),
        out_shape=[jax.ShapeDtypeStruct((NZ * (edge + HEAD), edge), f32)] * layer,
        compiler_params=pltpu.CompilerParams(vmem_limit_bytes=40 << 20),
        name="pick",
    )(rnd, place, codes, *arrays)


def overflow_round(rnd, place, pay, layer, per_round):
    row = per_round * pay.shape[1]
    line = [pay]
    for k in range(1, NZ):
        line.append(lax.ppermute(pay, AXES, [(z * layer + i, (z ^ k) * layer + i) for z in range(NZ) for i in range(layer)]))
    codes = jnp.stack([a[row] for a in line]).astype(jnp.int32)
    parts = pick(rnd, place, codes, line, layer, per_round)
    got = [parts[0]]
    for m in range(1, layer):
        pairs = [(z * layer + i, z * layer + (i ^ m)) for z in range(NZ) for i in range(layer)]
        got.append(lax.ppermute(parts[m], AXES, pairs))
    return got


def split_kernel(per_step, wide, source, both):
    edge = both.shape[1] // 2
    for c in range(per_step):
        for a in range(wide):
            x = source[pl.ds(c * edge * wide + a, edge, stride=wide), :]
            h = x.astype(bf16)
            both[c, :edge, a * edge : (a + 1) * edge] = h
            both[c, edge:, a * edge : (a + 1) * edge] = (x - h.astype(f32)).astype(bf16)


def split(integrals):
    rows, wide, edge = integrals.shape
    blocks = rows // edge
    per_step = 4
    return pl.pallas_call(
        functools.partial(split_kernel, per_step, wide),
        grid=(blocks // per_step,),
        in_specs=[pl.BlockSpec((per_step * edge * wide, edge), lambda i: (i, 0))],
        out_specs=pl.BlockSpec((per_step, 2 * edge, wide * edge), lambda i: (i, 0, 0)),
        out_shape=jax.ShapeDtypeStruct((blocks, 2 * edge, wide * edge), bf16),
        compiler_params=pltpu.CompilerParams(vmem_limit_bytes=40 << 20),
        cost_estimate=pl.CostEstimate(flops=0, bytes_accessed=2 * rows * wide * edge * 4, transcendentals=0),
        name="split",
    )(integrals.reshape(rows * wide, edge))


def product_kernel(layer, second, low_occ, occs, per_round, cols, own, init, rnd, place, table, *refs):
    sources = refs[: layer if second else 1]
    refs = refs[len(sources) :]
    both, refs = refs[0], refs[1:]
    if init:
        start_ref, refs = refs[0], refs[1:]
    out = refs[0]
    tiles, held, acc, queue, sem_t, sem_b, sem_i, sem_o = refs[1:]
    edge = both.shape[1] // 2
    wide = acc.shape[0]
    rows = occs * edge
    z, mine, x, core = place[0], place[1], place[2], place[3]

    if second:
        loads = [pltpu.make_async_copy(sources[m].at[pl.ds(0, NZ * edge), :], tiles.at[m], sem_t.at[m]) for m in range(layer)]
    else:
        loads = [pltpu.make_async_copy(sources[0].at[pl.ds(k * layer, layer)], tiles.at[pl.ds(k * layer, layer)], sem_t.at[k]) for k in range(NZ)]
    if init:
        loads.append(pltpu.make_async_copy(start_ref.at[:, pl.ds(low_occ * edge, rows), :], acc, sem_i))
    for load in loads:
        load.start()

    def listing(k, n):
        m, at = k // NZ, k % NZ
        code = table[k]
        if second:
            pair = ((code >> SHIFT) & MASK) - 1
            here = (code >> (2 * SHIFT)) - rnd[0] * per_round
            ok = (pair >= 0) & (here >= 0) & (here < per_round)
            where = m * NZ + at
        else:
            pair = (code & MASK) - 1
            ok = pair >= 0
            where = at * layer + (mine ^ m)
        p = pair // CV_DEV
        ok = ok & (p >= low_occ) & (p < low_occ + occs)

        @pl.when(ok)
        def _():
            queue[3 * n] = where
            queue[3 * n + 1] = p - low_occ
            queue[3 * n + 2] = pair % CV_DEV

        return n + ok.astype(jnp.int32)

    total = lax.fori_loop(0, layer * NZ, listing, jnp.int32(0))

    def fetch(n):
        slot = n % NBUF
        return pltpu.make_async_copy(both.at[queue[3 * n + 2]], held.at[slot], sem_b.at[slot])

    for n in range(NBUF - 1):

        @pl.when(n < total)
        def _():
            fetch(n).start()

    if not init:
        acc[...] = jnp.zeros_like(acc)
    for load in loads:
        load.wait()

    def step(n, c):
        @pl.when(n + NBUF - 1 < total)
        def _():
            fetch(n + NBUF - 1).start()

        fetch(n).wait()
        slot = n % NBUF
        where = queue[3 * n]
        if second:
            a = tiles[where // NZ, pl.ds(pl.multiple_of((where % NZ) * edge, edge), edge), :]
        else:
            a = tiles[where]
        ah = a.astype(bf16)
        al = (a - ah.astype(f32)).astype(bf16)
        dot = functools.partial(jnp.dot, preferred_element_type=f32)
        r = dot(jnp.concatenate([ah, ah], axis=1), held[slot]) + dot(al, held[slot, :edge, :])
        at = pl.ds(pl.multiple_of(queue[3 * n + 1] * edge, edge), edge)
        for k in range(wide):
            acc[k, at, :] += r[:, k * edge : (k + 1) * edge]
        return c

    lax.fori_loop(0, total, step, 0)
    stores = []
    if len(out.shape) == 3:
        stores.append(pltpu.make_async_copy(acc, out, sem_o.at[0]))
    else:
        chips = cols // 2
        for part in range(2):
            for j in range(chips):
                block = (lax.rem(x + j, chips) * 2 + (core ^ part)) * own
                stores.append(pltpu.make_async_copy(acc.at[pl.ds(block, own)], out.at[part, j], sem_o.at[part * chips + j]))
    for store in stores:
        store.start()
    for store in stores:
        store.wait()


def product(rnd, place, table, sources, both, start, layer, per_round, cols, own, low_occ, occs, scatter):
    second = len(sources) > 1
    edge = both.shape[1] // 2
    wide = both.shape[2] // edge
    rows = occs * edge
    chips = cols // 2
    out_shape = (2, chips, own, rows, edge) if scatter else (wide, rows, edge)
    tile_shape = (layer, NZ * edge, edge) if second else (layer * NZ, edge, edge)
    operands = list(sources) + [both] + ([start] if start is not None else [])
    return pl.pallas_call(
        functools.partial(product_kernel, layer, second, low_occ, occs, per_round, cols, own, start is not None),
        grid_spec=pltpu.PrefetchScalarGridSpec(
            num_scalar_prefetch=3,
            in_specs=[ANY] * len(operands),
            out_specs=ANY,
            scratch_shapes=[
                pltpu.VMEM(tile_shape, f32),
                pltpu.VMEM((NBUF, 2 * edge, wide * edge), bf16),
                pltpu.VMEM((wide, rows, edge), f32),
                pltpu.SMEM((3 * layer * NZ,), jnp.int32),
                pltpu.SemaphoreType.DMA((max(layer, NZ),)),
                pltpu.SemaphoreType.DMA((NBUF,)),
                pltpu.SemaphoreType.DMA,
                pltpu.SemaphoreType.DMA((2 * chips,)),
            ],
        ),
        out_shape=jax.ShapeDtypeStruct(out_shape, f32),
        compiler_params=pltpu.CompilerParams(vmem_limit_bytes=48 << 20),
        cost_estimate=pl.CostEstimate(flops=2 * layer * NZ * edge * edge * edge * wide, bytes_accessed=16 << 20, transcendentals=0),
        name="second_tiles" if second else "first_tiles",
    )(rnd, place, table, *operands)


def scatter_sum(parts, cols):
    chips = cols // 2
    got = lax.ppermute(parts[1], "col", [(c, c ^ 1) for c in range(cols)])
    total = parts[0, 0] + got[0]
    for j in range(1, chips):
        pairs = [(c, (c // 2 + j) % chips * 2 + c % 2) for c in range(cols)]
        total = total + lax.ppermute(parts[0, j] + got[j], "col", pairs)
    return total


def body(amplitudes, amp_owner, amp_occ, amp_vir, integrals):
    rows, cols = lax.axis_size("row"), lax.axis_size("col")
    devices = rows * cols
    layer = devices // NZ
    per_round = max(1, amplitudes.shape[0] // 8)
    own = integrals.shape[1] // cols
    edge = amplitudes.shape[1]
    row, col = lax.axis_index("row"), lax.axis_index("col")
    me = row * cols + col
    place = jnp.stack([me // layer, me % layer, col // 2, col % 2]).astype(jnp.int32)
    owner = amp_owner[:, 0]

    def packed(r):
        return pack(r, owner, amp_occ, amp_vir, amplitudes, devices, per_round)

    zero = jnp.zeros((1,), jnp.int32)
    send, pay = packed(zero)
    first = lax.all_to_all(send, AXES, split_axis=0, concat_axis=0, tiled=True)
    got = overflow_round(zero, place, pay, layer, per_round)
    both = split(integrals)
    heads = jnp.stack([g[NZ * edge :].reshape(NZ, HEAD, 128)[:, 0] for g in got]).astype(jnp.int32)
    table = lax.dynamic_index_in_dim(heads, me, 2, keepdims=False).reshape(-1)
    most = jnp.max(jnp.sum(((heads >> SHIFT) & MASK) > 0, axis=2, dtype=jnp.int32))
    rounds = (most + per_round - 1) // per_round

    def run(r, sources, start, low_occ, occs, scatter):
        return product(r, place, table, sources, both, start, layer, per_round, cols, own, low_occ, occs, scatter)

    start = run(zero, got, None, 0, OCC_DEV, False)
    step = OCC_DEV // GROUPS
    pieces = [scatter_sum(run(zero, [first], start, g * step, step, True), cols) for g in range(GROUPS)]
    out = jnp.concatenate(pieces, axis=1)

    def more(carry):
        r, total = carry
        at = jnp.reshape(r, (1,))
        again = overflow_round(at, place, packed(at)[1], layer, per_round)
        parts = run(at, again, None, 0, OCC_DEV, True)
        return r + 1, total + scatter_sum(parts, cols)

    return lax.while_loop(lambda c: c[0] < rounds, more, (jnp.int32(1), out))[1]


def solution(mesh):
    in_specs = (
        P(("row", "col"), None, None),
        P(("row", "col"), None),
        P(("row", "col")),
        P(("row", "col")),
        P("col", None, None),
    )
    out_specs = P("col", "row", None)
    return jax.shard_map(body, mesh=mesh, in_specs=in_specs, out_specs=out_specs, check_vma=False)
```

```python
import functools
import math

import jax
import jax.numpy as jnp
from jax import lax
from jax.experimental import pallas as pl
from jax.experimental.pallas import tpu as pltpu
from jax.sharding import PartitionSpec as P

CAP = 2
OCC_DEV = 12
CV_DEV = 32
CV_BITS = CV_DEV.bit_length() - 1
NZ = 4
PIECES = 4
HEAD = 8
SPANS = (5, 7)
SHIFT = 9
MASK = (1 << SHIFT) - 1
GROUP = 4
SLOTS = 4
AXES = ("row", "col")
ANY = pl.BlockSpec(memory_space=pl.ANY)
f32 = jnp.float32
bf16 = jnp.bfloat16


def room(*arrays):
    return sum(4 * math.prod(a) for a in arrays) + (6 << 20)


def pack_kernel(tiles, devices, per_round, rnd, owner, occ, vir, amp, send, pay, held, count, head, sem_in, sem_a, sem_b, sem_h):
    edge = amp.shape[1]
    piece = tiles // PIECES
    loads = [pltpu.make_async_copy(amp.at[pl.ds(i * piece, piece)], held.at[pl.ds(i * piece, piece)], sem_in.at[i]) for i in range(PIECES)]
    for load in loads:
        load.start()

    def clear(d, c):
        count[d] = 0
        head[0, d] = 0.0
        return c

    lax.fori_loop(0, devices, clear, 0, unroll=8)
    base = rnd[0] * per_round

    def first(t, d):
        return pltpu.make_async_copy(held.at[t], send.at[d], sem_a.at[d])

    def second(t, j):
        return pltpu.make_async_copy(held.at[t], pay.at[pl.ds(pl.multiple_of(j * edge, edge), edge), :], sem_b.at[j])

    def place_tile(t, j):
        o = owner[t]
        n = count[o]
        count[o] = n + 1
        pair = occ[t] * CV_DEV + vir[t] + 1
        here = j - base

        @pl.when(n == 0)
        def _():
            first(t, o).start()
            head[0, o] = pair.astype(f32)

        @pl.when(n > 0)
        def _():
            head[0, o] = head[0, o] + ((pair << SHIFT) + (j << (2 * SHIFT))).astype(f32)

        @pl.when((n > 0) & (here >= 0) & (here < per_round))
        def _():
            second(t, here).start()

        return j + (n > 0).astype(jnp.int32)

    total = jnp.int32(0)
    for i in range(PIECES):
        loads[i].wait()
        total = lax.fori_loop(i * piece, (i + 1) * piece, place_tile, total, unroll=4)
    copy = pltpu.make_async_copy(head, pay.at[pl.ds(per_round * edge, HEAD), :], sem_h)
    copy.start()

    for j in range(per_round):

        @pl.when(base + j < total)
        def _():
            second(0, j).wait()

    copy.wait()

    def settle(d, c):
        @pl.when(count[d] > 0)
        def _():
            first(0, d).wait()

        return c

    lax.fori_loop(0, devices, settle, 0, unroll=8)


def pack(rnd, owner, occ, vir, amp, devices, per_round):
    tiles, edge = amp.shape[:2]
    return pl.pallas_call(
        functools.partial(pack_kernel, tiles, devices, per_round),
        grid_spec=pltpu.PrefetchScalarGridSpec(
            num_scalar_prefetch=4,
            in_specs=[ANY],
            out_specs=[pl.BlockSpec(memory_space=pltpu.HBM), pl.BlockSpec(memory_space=pltpu.VMEM)],
            scratch_shapes=[
                pltpu.VMEM((tiles, edge, edge), f32),
                pltpu.SMEM((devices,), jnp.int32),
                pltpu.SMEM((HEAD, 128), f32),
                pltpu.SemaphoreType.DMA((PIECES,)),
                pltpu.SemaphoreType.DMA((devices,)),
                pltpu.SemaphoreType.DMA((per_round,)),
                pltpu.SemaphoreType.DMA,
            ],
        ),
        out_shape=[
            pltpu.HBM((devices, edge, edge), f32),
            jax.ShapeDtypeStruct((per_round * edge + HEAD, edge), f32),
        ],
        compiler_params=pltpu.CompilerParams(vmem_limit_bytes=room(amp.shape, (per_round * edge, edge))),
        name="pack",
    )(rnd, owner, occ, vir, amp)


def pick_kernel(layer, per_round, rnd, place, codes, *refs):
    line = refs[:NZ]
    outs = refs[NZ:]
    edge = line[0].shape[1]
    z, mine = place[0], place[1]
    for k in range(NZ):
        at = z ^ k
        head = line[k][pl.ds(per_round * edge, HEAD), :]
        for m in range(layer):
            code = codes[k, z * layer + (mine ^ m)]
            here = (code >> (2 * SHIFT)) - rnd[0] * per_round
            full = ((code >> SHIFT) & MASK) > 0

            @pl.when(full & (here >= 0) & (here < per_round))
            def _():
                rows = pl.ds(pl.multiple_of(here * edge, edge), edge)
                outs[m][pl.ds(pl.multiple_of(at * edge, edge), edge), :] = line[k][rows, :]

            outs[m][pl.ds(pl.multiple_of(NZ * edge + at * HEAD, HEAD), HEAD), :] = head


def pick(rnd, place, codes, arrays, layer, per_round):
    rows, edge = arrays[0].shape
    whole = pl.BlockSpec(memory_space=pltpu.VMEM)
    return pl.pallas_call(
        functools.partial(pick_kernel, layer, per_round),
        grid_spec=pltpu.PrefetchScalarGridSpec(
            num_scalar_prefetch=3,
            in_specs=[whole] * NZ,
            out_specs=[whole] * layer,
        ),
        out_shape=[jax.ShapeDtypeStruct((NZ * (edge + HEAD), edge), f32)] * layer,
        compiler_params=pltpu.CompilerParams(vmem_limit_bytes=room((NZ, rows, edge), (layer, NZ * (edge + HEAD), edge))),
        name="pick",
    )(rnd, place, codes, *arrays)


def overflow_round(rnd, place, pay, layer, per_round, tie):
    row = per_round * pay.shape[1]

    def along(k):
        return [(z * layer + i, (z ^ k) * layer + i) for z in range(NZ) for i in range(layer)]

    cross = lax.ppermute(pay, AXES, along(2))
    near = lax.ppermute(pay, AXES, along(1))
    cross, tie = lax.optimization_barrier((cross, tie))
    line = [pay, near, cross, lax.ppermute(cross, AXES, along(1))]
    codes = jnp.stack([a[row] for a in line]).astype(jnp.int32)
    parts = pick(rnd, place, codes, line, layer, per_round)
    got = [parts[0]]
    for m in range(1, layer):
        pairs = [(z * layer + i, z * layer + (i ^ m)) for z in range(NZ) for i in range(layer)]
        got.append(lax.ppermute(parts[m], AXES, pairs))
    return got, tie


def split_kernel(per_step, wide, source, both):
    edge = both.shape[1] // 2
    for c in range(per_step):
        for a in range(wide):
            x = source[pl.ds(c * edge * wide + a, edge, stride=wide), :]
            h = x.astype(bf16)
            both[c, :edge, a * edge : (a + 1) * edge] = h
            both[c, edge:, a * edge : (a + 1) * edge] = (x - h.astype(f32)).astype(bf16)


def split(integrals):
    rows, wide, edge = integrals.shape
    blocks = rows // edge
    per_step = 4
    return pl.pallas_call(
        functools.partial(split_kernel, per_step, wide),
        grid=(blocks // per_step,),
        in_specs=[pl.BlockSpec((per_step * edge * wide, edge), lambda i: (i, 0))],
        out_specs=pl.BlockSpec((per_step, 2 * edge, wide * edge), lambda i: (i, 0, 0)),
        out_shape=jax.ShapeDtypeStruct((blocks, 2 * edge, wide * edge), bf16),
        compiler_params=pltpu.CompilerParams(vmem_limit_bytes=16 << 20),
        cost_estimate=pl.CostEstimate(flops=0, bytes_accessed=2 * rows * wide * edge * 4, transcendentals=0),
        name="split",
    )(integrals.reshape(rows * wide, edge))


def product_kernel(layer, firsts, low_occ, occs, per_round, cols, own, rnd, place, table, *refs):
    sources, refs = refs[:layer], refs[layer:]
    if firsts:
        first, refs = refs[0], refs[1:]
    both, keep, give, tiles, held, acc, queue, sem_t, sem_b, sem_o = refs
    edge = both.shape[1] // 2
    wide = acc.shape[0]
    count = layer * NZ
    z, mine, x, core = place[0], place[1], place[2], place[3]
    dot = functools.partial(jnp.dot, preferred_element_type=f32)

    slots = held.shape[0]

    def enter(base, n, where, number, ok):
        pair = number - 1
        p = pair >> CV_BITS
        queue[3 * (base + n)] = where
        queue[3 * (base + n) + 1] = p - low_occ
        queue[3 * (base + n) + 2] = pair & (CV_DEV - 1)
        ok = ok & (number > 0) & (p >= low_occ) & (p < low_occ + occs)
        return ok, n + ok.astype(jnp.int32)

    def pad(n):
        for u in range(3 * GROUP):
            queue[3 * n + u] = 0

    def fetch(g, u):
        slot = lax.rem(g, slots)
        return pltpu.make_async_copy(both.at[queue[3 * (g * GROUP + u) + 2]], held.at[slot, u], sem_b.at[slot, u])

    def ahead(g, groups):
        @pl.when(g < groups)
        def _():
            for u in range(GROUP):
                fetch(g, u).start()

    def work(ref, low, high, base, total, groups):
        def step(g, c):
            ahead(g + slots - 1, groups)
            for u in range(GROUP):
                fetch(g, u).wait()
            for u in range(GROUP):
                n = g * GROUP + u
                a = jnp.where(n - base < total, ref[queue[3 * n]], 0.0)
                ah = a.astype(bf16)
                al = (a - ah.astype(f32)).astype(bf16)
                b = held.at[lax.rem(g, slots), u]
                r = dot(jnp.concatenate([ah, ah], axis=1), b[...]) + dot(al, b[:edge, :])
                at = pl.ds(pl.multiple_of(queue[3 * n + 1] * edge, edge), edge)
                for k in range(wide):
                    acc[k, at, :] += r[:, k * edge : (k + 1) * edge]
            return c

        lax.fori_loop(low, high, step, 0)

    total = jnp.int32(0)
    if firsts:

        def listing(i, n):
            m, at = i // NZ, i % NZ
            return enter(0, n, at * layer + (mine ^ m), table[i] & MASK, True)[1]

        total = lax.fori_loop(0, count, listing, total, unroll=4)
        pad(total)
    early = (total + GROUP - 1) // GROUP
    for g in range(slots - 1):
        ahead(jnp.int32(g), early)

    seconds = jnp.int32(0)
    for m in range(layer):
        for k in range(NZ):
            code = table[m * NZ + k]
            here = (code >> (2 * SHIFT)) - rnd[0] * per_round
            ok, more = enter(GROUP * early, seconds, seconds, (code >> SHIFT) & MASK, (here >= 0) & (here < per_round))

            @pl.when(ok)
            def _():
                pltpu.make_async_copy(sources[m].at[pl.ds(k * edge, edge), :], tiles.at[seconds], sem_t.at[seconds]).start()

            seconds = more
    pad(GROUP * early + seconds)
    groups = early + (seconds + GROUP - 1) // GROUP
    for g in range(slots - 1):

        @pl.when(g >= early)
        def _():
            ahead(jnp.int32(g), groups)

    acc[...] = jnp.zeros_like(acc)
    if firsts:
        work(first, 0, early, 0, total, groups)

    def arrive(n, c):
        pltpu.make_async_copy(sources[0].at[pl.ds(0, edge), :], tiles.at[n], sem_t.at[n]).wait()
        return c

    lax.fori_loop(0, seconds, arrive, 0)
    work(tiles, early, groups, GROUP * early, seconds, groups)

    chips = cols // 2
    stores = []
    for part, out in enumerate((keep, give)):
        for j in range(chips):
            block = (lax.rem(x + j, chips) * 2 + (core ^ part)) * own
            stores.append(pltpu.make_async_copy(acc.at[pl.ds(block, own)], out.at[j], sem_o.at[part * chips + j]))
    for store in stores:
        store.start()
    for store in stores:
        store.wait()


def product(rnd, place, table, second, first, both, layer, per_round, cols, own, low_occ, occs):
    edge = both.shape[1] // 2
    wide = both.shape[2] // edge
    rows = occs * edge
    chips = cols // 2
    count = layer * NZ
    firsts = first is not None
    operands = [pltpu.with_memory_space_constraint(a, pltpu.HBM) for a in second]
    if firsts:
        operands.append(pltpu.with_memory_space_constraint(first, pltpu.VMEM))
    out = jax.ShapeDtypeStruct((chips, own, rows, edge), f32)
    return pl.pallas_call(
        functools.partial(product_kernel, layer, firsts, low_occ, occs, per_round, cols, own),
        grid_spec=pltpu.PrefetchScalarGridSpec(
            num_scalar_prefetch=3,
            in_specs=[ANY] * len(second) + [pl.BlockSpec(memory_space=pltpu.VMEM)] * firsts + [ANY],
            out_specs=[ANY, ANY],
            scratch_shapes=[
                pltpu.VMEM((count, edge, edge), f32),
                pltpu.VMEM((SLOTS, GROUP, 2 * edge, wide * edge), bf16),
                pltpu.VMEM((wide, rows, edge), f32),
                pltpu.SMEM((6 * (count + GROUP),), jnp.int32),
                pltpu.SemaphoreType.DMA((count,)),
                pltpu.SemaphoreType.DMA((SLOTS, GROUP)),
                pltpu.SemaphoreType.DMA((2 * chips,)),
            ],
        ),
        out_shape=[out, out],
        compiler_params=pltpu.CompilerParams(vmem_limit_bytes=room((count, edge, edge), (SLOTS * GROUP, edge, wide * edge), (wide, rows, edge), (GROUP, edge, 2 * wide * edge))),
        cost_estimate=pl.CostEstimate(flops=4 * count * edge * edge * edge * wide, bytes_accessed=16 << 20, transcendentals=0),
        name="product",
    )(rnd, place, table, *operands, both)


def chip_sum(keep, give, cols):
    got = lax.ppermute(give, "col", [(c, c ^ 1) for c in range(cols)])
    return [keep[j] + got[j] for j in range(cols // 2)]


def exchange(sums, cols):
    chips = cols // 2
    return [lax.ppermute(sums[j], "col", [(c, (c // 2 + j) % chips * 2 + c % 2) for c in range(cols)]) for j in range(1, chips)]


def body(amplitudes, amp_owner, amp_occ, amp_vir, integrals):
    rows, cols = lax.axis_size("row"), lax.axis_size("col")
    devices = rows * cols
    layer = devices // NZ
    per_round = max(1, amplitudes.shape[0] // 8)
    own = integrals.shape[1] // cols
    edge = amplitudes.shape[1]
    row, col = lax.axis_index("row"), lax.axis_index("col")
    me = row * cols + col
    place = jnp.stack([me // layer, me % layer, col // 2, col % 2]).astype(jnp.int32)
    owner = amp_owner[:, 0]

    def packed(r):
        return pack(r, owner, amp_occ, amp_vir, amplitudes, devices, per_round)

    zero = jnp.zeros((1,), jnp.int32)
    send, pay = packed(zero)
    first = lax.all_to_all(send, AXES, split_axis=0, concat_axis=0, tiled=True)
    got, both = overflow_round(zero, place, pay, layer, per_round, split(integrals))
    heads = jnp.stack([g[NZ * edge :].reshape(NZ, HEAD, 128)[:, 0] for g in got]).astype(jnp.int32)
    table = lax.dynamic_index_in_dim(heads, me, 2, keepdims=False).reshape(-1)
    most = jnp.max(jnp.sum(((heads >> SHIFT) & MASK) > 0, axis=2, dtype=jnp.int32))
    rounds = (most + per_round - 1) // per_round

    def run(r, table, second, firsts, low_occ, occs):
        return product(r, place, table, second, firsts, both, layer, per_round, cols, own, low_occ, occs)

    pieces, moved = [], None
    for g, occs in enumerate(SPANS):
        keep, give = run(zero, table, got, first, sum(SPANS[:g]), occs)
        if moved is not None:
            give, moved = lax.optimization_barrier((give, moved))
            pieces.append(functools.reduce(jnp.add, moved, sums[0]))
        sums = chip_sum(keep, give, cols)
        sums, table = lax.optimization_barrier((sums, table))
        moved = exchange(sums, cols)
    pieces.append(functools.reduce(jnp.add, moved, sums[0]))
    out = jnp.concatenate(pieces, axis=1)

    def more(carry):
        r, total = carry
        at = jnp.reshape(r, (1,))
        again, _ = overflow_round(at, place, packed(at)[1], layer, per_round, place)
        sums = chip_sum(*run(at, table, again, None, 0, OCC_DEV), cols)
        return r + 1, functools.reduce(jnp.add, exchange(sums, cols), total + sums[0])

    return lax.while_loop(lambda c: c[0] < rounds, more, (jnp.int32(1), out))[1]


def solution(mesh):
    in_specs = (
        P(("row", "col"), None, None),
        P(("row", "col"), None),
        P(("row", "col")),
        P(("row", "col")),
        P("col", None, None),
    )
    out_specs = P("col", "row", None)
    return jax.shard_map(body, mesh=mesh, in_specs=in_specs, out_specs=out_specs, check_vma=False)
```

```python
import functools
import math

import jax
import jax.numpy as jnp
from jax import lax
from jax.experimental import pallas as pl
from jax.experimental.pallas import tpu as pltpu
from jax.sharding import PartitionSpec as P

CAP = 2
OCC_DEV = 12
CV_DEV = 32
CV_BITS = CV_DEV.bit_length() - 1
NZ = 4
PIECES = 4
HEAD = 8
SPANS = (5, 7)
SHIFT = 9
MASK = (1 << SHIFT) - 1
GROUP = 4
SLOTS = 4
AXES = ("row", "col")
ANY = pl.BlockSpec(memory_space=pl.ANY)
f32 = jnp.float32
bf16 = jnp.bfloat16


def room(*arrays):
    return sum(4 * math.prod(a) for a in arrays) + (6 << 20)


def pack_kernel(tiles, devices, per_round, rnd, owner, occ, vir, amp, send, pay, held, count, head, sem_in, sem_a, sem_b, sem_h):
    edge = amp.shape[1]
    piece = tiles // PIECES
    loads = [pltpu.make_async_copy(amp.at[pl.ds(i * piece, piece)], held.at[pl.ds(i * piece, piece)], sem_in.at[i]) for i in range(PIECES)]
    for load in loads:
        load.start()

    def clear(d, c):
        count[d] = 0
        head[0, d] = 0.0
        return c

    lax.fori_loop(0, devices, clear, 0, unroll=8)
    base = rnd[0] * per_round

    def first(t, d):
        return pltpu.make_async_copy(held.at[t], send.at[d], sem_a.at[d])

    def second(t, j):
        return pltpu.make_async_copy(held.at[t], pay.at[pl.ds(pl.multiple_of(j * edge, edge), edge), :], sem_b.at[j])

    def place_tile(t, j):
        o = owner[t]
        n = count[o]
        count[o] = n + 1
        pair = occ[t] * CV_DEV + vir[t] + 1
        here = j - base

        @pl.when(n == 0)
        def _():
            first(t, o).start()
            head[0, o] = pair.astype(f32)

        @pl.when(n > 0)
        def _():
            head[0, o] = head[0, o] + ((pair << SHIFT) + (j << (2 * SHIFT))).astype(f32)

        @pl.when((n > 0) & (here >= 0) & (here < per_round))
        def _():
            second(t, here).start()

        return j + (n > 0).astype(jnp.int32)

    total = jnp.int32(0)
    for i in range(PIECES):
        loads[i].wait()
        total = lax.fori_loop(i * piece, (i + 1) * piece, place_tile, total, unroll=4)
    copy = pltpu.make_async_copy(head, pay.at[pl.ds(per_round * edge, HEAD), :], sem_h)
    copy.start()

    for j in range(per_round):

        @pl.when(base + j < total)
        def _():
            second(0, j).wait()

    copy.wait()

    def settle(d, c):
        @pl.when(count[d] > 0)
        def _():
            first(0, d).wait()

        return c

    lax.fori_loop(0, devices, settle, 0, unroll=8)


def pack(rnd, owner, occ, vir, amp, devices, per_round):
    tiles, edge = amp.shape[:2]
    return pl.pallas_call(
        functools.partial(pack_kernel, tiles, devices, per_round),
        grid_spec=pltpu.PrefetchScalarGridSpec(
            num_scalar_prefetch=4,
            in_specs=[ANY],
            out_specs=[pl.BlockSpec(memory_space=pltpu.HBM), pl.BlockSpec(memory_space=pltpu.VMEM)],
            scratch_shapes=[
                pltpu.VMEM((tiles, edge, edge), f32),
                pltpu.SMEM((devices,), jnp.int32),
                pltpu.SMEM((HEAD, 128), f32),
                pltpu.SemaphoreType.DMA((PIECES,)),
                pltpu.SemaphoreType.DMA((devices,)),
                pltpu.SemaphoreType.DMA((per_round,)),
                pltpu.SemaphoreType.DMA,
            ],
        ),
        out_shape=[
            pltpu.HBM((devices, edge, edge), f32),
            jax.ShapeDtypeStruct((per_round * edge + HEAD, edge), f32),
        ],
        compiler_params=pltpu.CompilerParams(vmem_limit_bytes=room(amp.shape, (per_round * edge, edge))),
        name="pack",
    )(rnd, owner, occ, vir, amp)


def pick_kernel(layer, per_round, rnd, place, codes, *refs):
    line = refs[:NZ]
    outs = refs[NZ:]
    edge = line[0].shape[1]
    z, mine = place[0], place[1]
    for k in range(NZ):
        at = z ^ k
        head = line[k][pl.ds(per_round * edge, HEAD), :]
        for m in range(layer):
            code = codes[k, z * layer + (mine ^ m)]
            here = (code >> (2 * SHIFT)) - rnd[0] * per_round
            full = ((code >> SHIFT) & MASK) > 0

            @pl.when(full & (here >= 0) & (here < per_round))
            def _():
                rows = pl.ds(pl.multiple_of(here * edge, edge), edge)
                outs[m][pl.ds(pl.multiple_of(at * edge, edge), edge), :] = line[k][rows, :]

            outs[m][pl.ds(pl.multiple_of(NZ * edge + at * HEAD, HEAD), HEAD), :] = head


def pick(rnd, place, codes, arrays, layer, per_round):
    rows, edge = arrays[0].shape
    whole = pl.BlockSpec(memory_space=pltpu.VMEM)
    return pl.pallas_call(
        functools.partial(pick_kernel, layer, per_round),
        grid_spec=pltpu.PrefetchScalarGridSpec(
            num_scalar_prefetch=3,
            in_specs=[whole] * NZ,
            out_specs=[whole] * layer,
        ),
        out_shape=[jax.ShapeDtypeStruct((NZ * (edge + HEAD), edge), f32)] * layer,
        compiler_params=pltpu.CompilerParams(vmem_limit_bytes=room((NZ, rows, edge), (layer, NZ * (edge + HEAD), edge))),
        name="pick",
    )(rnd, place, codes, *arrays)


def overflow_round(rnd, place, pay, layer, per_round, tie):
    row = per_round * pay.shape[1]

    def along(k):
        return [(z * layer + i, (z ^ k) * layer + i) for z in range(NZ) for i in range(layer)]

    cross = lax.ppermute(pay, AXES, along(2))
    near = lax.ppermute(pay, AXES, along(1))
    cross, tie = lax.optimization_barrier((cross, tie))
    line = [pay, near, cross, lax.ppermute(cross, AXES, along(1))]
    codes = jnp.stack([a[row] for a in line]).astype(jnp.int32)
    parts = pick(rnd, place, codes, line, layer, per_round)
    got = [parts[0]]
    for m in range(1, layer):
        pairs = [(z * layer + i, z * layer + (i ^ m)) for z in range(NZ) for i in range(layer)]
        got.append(lax.ppermute(parts[m], AXES, pairs))
    return got, tie


def block_order(place, wide, cols):
    chips, own = cols // 2, wide // cols
    x, core = place[2], place[3]
    return [(lax.rem(x + j, chips) * 2 + (core ^ part)) * own + o for part in range(2) for j in range(chips) for o in range(own)]


def split_kernel(per_step, wide, cols, place, source, both):
    edge = both.shape[1] // 2
    order = block_order(place, wide, cols)
    for c in range(per_step):
        for a in range(wide):
            x = source[pl.ds(c * edge * wide + order[a], edge, stride=wide), :]
            h = x.astype(bf16)
            both[c, :edge, a * edge : (a + 1) * edge] = h
            both[c, edge:, a * edge : (a + 1) * edge] = (x - h.astype(f32)).astype(bf16)


def split(place, integrals, cols):
    rows, wide, edge = integrals.shape
    blocks = rows // edge
    per_step = 4
    return pl.pallas_call(
        functools.partial(split_kernel, per_step, wide, cols),
        grid_spec=pltpu.PrefetchScalarGridSpec(
            num_scalar_prefetch=1,
            grid=(blocks // per_step,),
            in_specs=[pl.BlockSpec((per_step * edge * wide, edge), lambda i, at: (i, 0))],
            out_specs=pl.BlockSpec((per_step, 2 * edge, wide * edge), lambda i, at: (i, 0, 0)),
        ),
        out_shape=jax.ShapeDtypeStruct((blocks, 2 * edge, wide * edge), bf16),
        compiler_params=pltpu.CompilerParams(vmem_limit_bytes=16 << 20),
        cost_estimate=pl.CostEstimate(flops=0, bytes_accessed=2 * rows * wide * edge * 4, transcendentals=0),
        name="split",
    )(place, integrals.reshape(rows * wide, edge))


def product_kernel(layer, firsts, low_occ, occs, per_round, cols, own, rnd, place, table, *refs):
    sources, refs = refs[:layer], refs[layer:]
    if firsts:
        first, refs = refs[0], refs[1:]
    both, keep, give, tiles, held, queue, sem_t, sem_b = refs
    edge = both.shape[1] // 2
    wide = both.shape[2] // edge
    count = layer * NZ
    blocks = [(out, j, o) for out in (keep, give) for j in range(cols // 2) for o in range(own)]
    mine = place[1]
    dot = functools.partial(jnp.dot, preferred_element_type=f32)

    slots = held.shape[0]

    def enter(base, n, where, number, ok):
        pair = number - 1
        p = pair >> CV_BITS
        queue[3 * (base + n)] = where
        queue[3 * (base + n) + 1] = p - low_occ
        queue[3 * (base + n) + 2] = pair & (CV_DEV - 1)
        ok = ok & (number > 0) & (p >= low_occ) & (p < low_occ + occs)
        return ok, n + ok.astype(jnp.int32)

    def pad(n):
        for u in range(3 * GROUP):
            queue[3 * n + u] = 0

    def fetch(g, u):
        slot = lax.rem(g, slots)
        return pltpu.make_async_copy(both.at[queue[3 * (g * GROUP + u) + 2]], held.at[slot, u], sem_b.at[slot, u])

    def ahead(g, groups):
        @pl.when(g < groups)
        def _():
            for u in range(GROUP):
                fetch(g, u).start()

    def work(ref, low, high, base, total, groups):
        def step(g, c):
            ahead(g + slots - 1, groups)
            for u in range(GROUP):
                fetch(g, u).wait()
            for u in range(GROUP):
                n = g * GROUP + u
                a = jnp.where(n - base < total, ref[queue[3 * n]], 0.0)
                ah = a.astype(bf16)
                al = (a - ah.astype(f32)).astype(bf16)
                b = held.at[lax.rem(g, slots), u]
                r = dot(jnp.concatenate([ah, ah], axis=1), b[...]) + dot(al, b[:edge, :])
                at = pl.ds(pl.multiple_of(queue[3 * n + 1] * edge, edge), edge)
                for k, (out, j, o) in enumerate(blocks):
                    out[j, o, at, :] += r[:, k * edge : (k + 1) * edge]
            return c

        lax.fori_loop(low, high, step, 0)

    total = jnp.int32(0)
    if firsts:

        def listing(i, n):
            m, at = i // NZ, i % NZ
            return enter(0, n, at * layer + (mine ^ m), table[i] & MASK, True)[1]

        total = lax.fori_loop(0, count, listing, total, unroll=4)
        pad(total)
    early = (total + GROUP - 1) // GROUP
    for g in range(slots - 1):
        ahead(jnp.int32(g), early)

    seconds = jnp.int32(0)
    for m in range(layer):
        for k in range(NZ):
            code = table[m * NZ + k]
            here = (code >> (2 * SHIFT)) - rnd[0] * per_round
            ok, more = enter(GROUP * early, seconds, seconds, (code >> SHIFT) & MASK, (here >= 0) & (here < per_round))

            @pl.when(ok)
            def _():
                pltpu.make_async_copy(sources[m].at[pl.ds(k * edge, edge), :], tiles.at[seconds], sem_t.at[seconds]).start()

            seconds = more
    pad(GROUP * early + seconds)
    groups = early + (seconds + GROUP - 1) // GROUP
    for g in range(slots - 1):

        @pl.when(g >= early)
        def _():
            ahead(jnp.int32(g), groups)

    keep[...] = jnp.zeros_like(keep)
    give[...] = jnp.zeros_like(give)
    if firsts:
        work(first, 0, early, 0, total, groups)

    def arrive(n, c):
        pltpu.make_async_copy(sources[0].at[pl.ds(0, edge), :], tiles.at[n], sem_t.at[n]).wait()
        return c

    lax.fori_loop(0, seconds, arrive, 0)
    work(tiles, early, groups, GROUP * early, seconds, groups)


def product(rnd, place, table, second, first, both, layer, per_round, cols, own, low_occ, occs):
    edge = both.shape[1] // 2
    wide = both.shape[2] // edge
    rows = occs * edge
    chips = cols // 2
    count = layer * NZ
    firsts = first is not None
    operands = [pltpu.with_memory_space_constraint(a, pltpu.HBM) for a in second]
    if firsts:
        operands.append(pltpu.with_memory_space_constraint(first, pltpu.VMEM))
    out = pltpu.VMEM((chips, own, rows, edge), f32)
    return pl.pallas_call(
        functools.partial(product_kernel, layer, firsts, low_occ, occs, per_round, cols, own),
        grid_spec=pltpu.PrefetchScalarGridSpec(
            num_scalar_prefetch=3,
            in_specs=[ANY] * len(second) + [pl.BlockSpec(memory_space=pltpu.VMEM)] * firsts + [ANY],
            out_specs=[pl.BlockSpec(memory_space=pltpu.VMEM)] * 2,
            scratch_shapes=[
                pltpu.VMEM((count, edge, edge), f32),
                pltpu.VMEM((SLOTS, GROUP, 2 * edge, wide * edge), bf16),
                pltpu.SMEM((6 * (count + GROUP),), jnp.int32),
                pltpu.SemaphoreType.DMA((count,)),
                pltpu.SemaphoreType.DMA((SLOTS, GROUP)),
            ],
        ),
        out_shape=[out, out],
        compiler_params=pltpu.CompilerParams(vmem_limit_bytes=room((count, edge, edge), (SLOTS * GROUP, edge, wide * edge), (wide, rows, edge), (GROUP, edge, 2 * wide * edge))),
        cost_estimate=pl.CostEstimate(flops=4 * count * edge * edge * edge * wide, bytes_accessed=16 << 20, transcendentals=0),
        name="product",
    )(rnd, place, table, *operands, both)


def chip_sum(keep, give, cols):
    got = lax.ppermute(give, "col", [(c, c ^ 1) for c in range(cols)])
    return [keep[j] + got[j] for j in range(cols // 2)]


def exchange(sums, cols):
    chips = cols // 2
    return [lax.ppermute(sums[j], "col", [(c, (c // 2 + j) % chips * 2 + c % 2) for c in range(cols)]) for j in range(1, chips)]


def body(amplitudes, amp_owner, amp_occ, amp_vir, integrals):
    rows, cols = lax.axis_size("row"), lax.axis_size("col")
    devices = rows * cols
    layer = devices // NZ
    per_round = max(1, amplitudes.shape[0] // 8)
    own = integrals.shape[1] // cols
    edge = amplitudes.shape[1]
    row, col = lax.axis_index("row"), lax.axis_index("col")
    me = row * cols + col
    place = jnp.stack([me // layer, me % layer, col // 2, col % 2]).astype(jnp.int32)
    owner = amp_owner[:, 0]

    def packed(r):
        return pack(r, owner, amp_occ, amp_vir, amplitudes, devices, per_round)

    zero = jnp.zeros((1,), jnp.int32)
    send, pay = packed(zero)
    first = lax.all_to_all(send, AXES, split_axis=0, concat_axis=0, tiled=True)
    got, both = overflow_round(zero, place, pay, layer, per_round, split(place, integrals, cols))
    heads = jnp.stack([g[NZ * edge :].reshape(NZ, HEAD, 128)[:, 0] for g in got]).astype(jnp.int32)
    table = lax.dynamic_index_in_dim(heads, me, 2, keepdims=False).reshape(-1)
    most = jnp.max(jnp.sum(((heads >> SHIFT) & MASK) > 0, axis=2, dtype=jnp.int32))
    rounds = (most + per_round - 1) // per_round

    def run(r, table, second, firsts, low_occ, occs):
        return product(r, place, table, second, firsts, both, layer, per_round, cols, own, low_occ, occs)

    pieces, moved = [], None
    for g, occs in enumerate(SPANS):
        keep, give = run(zero, table, got, first, sum(SPANS[:g]), occs)
        if moved is not None:
            give, moved = lax.optimization_barrier((give, moved))
            pieces.append(functools.reduce(jnp.add, moved, sums[0]))
        sums = chip_sum(keep, give, cols)
        sums, table = lax.optimization_barrier((sums, table))
        moved = exchange(sums, cols)
    pieces.append(functools.reduce(jnp.add, moved, sums[0]))
    out = jnp.concatenate(pieces, axis=1)

    def more(carry):
        r, total = carry
        at = jnp.reshape(r, (1,))
        again, _ = overflow_round(at, place, packed(at)[1], layer, per_round, place)
        sums = chip_sum(*run(at, table, again, None, 0, OCC_DEV), cols)
        return r + 1, functools.reduce(jnp.add, exchange(sums, cols), total + sums[0])

    return lax.while_loop(lambda c: c[0] < rounds, more, (jnp.int32(1), out))[1]


def solution(mesh):
    in_specs = (
        P(("row", "col"), None, None),
        P(("row", "col"), None),
        P(("row", "col")),
        P(("row", "col")),
        P("col", None, None),
    )
    out_specs = P("col", "row", None)
    return jax.shard_map(body, mesh=mesh, in_specs=in_specs, out_specs=out_specs, check_vma=False)
```

```python
import functools
import math

import jax
import jax.numpy as jnp
from jax import lax
from jax.experimental import pallas as pl
from jax.experimental.pallas import tpu as pltpu
from jax.sharding import PartitionSpec as P

CAP = 2
OCC_DEV = 12
CV_DEV = 32
CV_BITS = CV_DEV.bit_length() - 1
NZ = 4
PIECES = 4
HEAD = 8
SPANS = (5, 7)
SHIFT = 9
MASK = (1 << SHIFT) - 1
GROUP = 4
SLOTS = 4
AXES = ("row", "col")
ANY = pl.BlockSpec(memory_space=pl.ANY)
f32 = jnp.float32
bf16 = jnp.bfloat16


def room(*arrays):
    return sum(4 * math.prod(a) for a in arrays) + (6 << 20)


def pack_kernel(tiles, devices, per_round, rnd, owner, occ, vir, amp, send, pay, held, count, head, sem_in, sem_a, sem_b, sem_h):
    edge = amp.shape[1]
    piece = tiles // PIECES
    loads = [pltpu.make_async_copy(amp.at[pl.ds(i * piece, piece)], held.at[pl.ds(i * piece, piece)], sem_in.at[i]) for i in range(PIECES)]
    for load in loads:
        load.start()

    def clear(d, c):
        count[d] = 0
        head[0, d] = 0.0
        return c

    lax.fori_loop(0, devices, clear, 0, unroll=8)
    base = rnd[0] * per_round

    def first(t, d):
        return pltpu.make_async_copy(held.at[t], send.at[d], sem_a.at[d])

    def second(t, j):
        return pltpu.make_async_copy(held.at[t], pay.at[pl.ds(pl.multiple_of(j * edge, edge), edge), :], sem_b.at[j])

    def place_tile(t, j):
        o = owner[t]
        n = count[o]
        count[o] = n + 1
        pair = occ[t] * CV_DEV + vir[t] + 1
        here = j - base

        @pl.when(n == 0)
        def _():
            first(t, o).start()
            head[0, o] = pair.astype(f32)

        @pl.when(n > 0)
        def _():
            head[0, o] = head[0, o] + ((pair << SHIFT) + (j << (2 * SHIFT))).astype(f32)

        @pl.when((n > 0) & (here >= 0) & (here < per_round))
        def _():
            second(t, here).start()

        return j + (n > 0).astype(jnp.int32)

    total = jnp.int32(0)
    for i in range(PIECES):
        loads[i].wait()
        total = lax.fori_loop(i * piece, (i + 1) * piece, place_tile, total, unroll=4)
    copy = pltpu.make_async_copy(head, pay.at[pl.ds(per_round * edge, HEAD), :], sem_h)
    copy.start()

    for j in range(per_round):

        @pl.when(base + j < total)
        def _():
            second(0, j).wait()

    copy.wait()

    def settle(d, c):
        @pl.when(count[d] > 0)
        def _():
            first(0, d).wait()

        return c

    lax.fori_loop(0, devices, settle, 0, unroll=8)


def pack(rnd, owner, occ, vir, amp, devices, per_round):
    tiles, edge = amp.shape[:2]
    return pl.pallas_call(
        functools.partial(pack_kernel, tiles, devices, per_round),
        grid_spec=pltpu.PrefetchScalarGridSpec(
            num_scalar_prefetch=4,
            in_specs=[ANY],
            out_specs=[pl.BlockSpec(memory_space=pltpu.HBM), pl.BlockSpec(memory_space=pltpu.VMEM)],
            scratch_shapes=[
                pltpu.VMEM((tiles, edge, edge), f32),
                pltpu.SMEM((devices,), jnp.int32),
                pltpu.SMEM((HEAD, 128), f32),
                pltpu.SemaphoreType.DMA((PIECES,)),
                pltpu.SemaphoreType.DMA((devices,)),
                pltpu.SemaphoreType.DMA((per_round,)),
                pltpu.SemaphoreType.DMA,
            ],
        ),
        out_shape=[
            pltpu.HBM((devices, edge, edge), f32),
            jax.ShapeDtypeStruct((per_round * edge + HEAD, edge), f32),
        ],
        compiler_params=pltpu.CompilerParams(vmem_limit_bytes=room(amp.shape, (per_round * edge, edge))),
        name="pack",
    )(rnd, owner, occ, vir, amp)


def pick_kernel(layer, per_round, rnd, place, codes, *refs):
    line = refs[:NZ]
    outs = refs[NZ:]
    edge = line[0].shape[1]
    z, mine = place[0], place[1]
    for k in range(NZ):
        at = z ^ k
        head = line[k][pl.ds(per_round * edge, HEAD), :]
        for m in range(layer):
            code = codes[k, z * layer + (mine ^ m)]
            here = (code >> (2 * SHIFT)) - rnd[0] * per_round
            full = ((code >> SHIFT) & MASK) > 0

            @pl.when(full & (here >= 0) & (here < per_round))
            def _():
                rows = pl.ds(pl.multiple_of(here * edge, edge), edge)
                outs[m][pl.ds(pl.multiple_of(at * edge, edge), edge), :] = line[k][rows, :]

            outs[m][pl.ds(pl.multiple_of(NZ * edge + at * HEAD, HEAD), HEAD), :] = head


def pick(rnd, place, codes, arrays, layer, per_round):
    rows, edge = arrays[0].shape
    whole = pl.BlockSpec(memory_space=pltpu.VMEM)
    return pl.pallas_call(
        functools.partial(pick_kernel, layer, per_round),
        grid_spec=pltpu.PrefetchScalarGridSpec(
            num_scalar_prefetch=3,
            in_specs=[whole] * NZ,
            out_specs=[whole] * layer,
        ),
        out_shape=[jax.ShapeDtypeStruct((NZ * (edge + HEAD), edge), f32)] * layer,
        compiler_params=pltpu.CompilerParams(vmem_limit_bytes=room((NZ, rows, edge), (layer, NZ * (edge + HEAD), edge))),
        name="pick",
    )(rnd, place, codes, *arrays)


def overflow_round(rnd, place, pay, layer, per_round, tie):
    row = per_round * pay.shape[1]

    def along(k):
        return [(z * layer + i, (z ^ k) * layer + i) for z in range(NZ) for i in range(layer)]

    cross = lax.ppermute(pay, AXES, along(2))
    near = lax.ppermute(pay, AXES, along(1))
    cross, tie = lax.optimization_barrier((cross, tie))
    line = [pay, near, cross, lax.ppermute(cross, AXES, along(1))]
    codes = jnp.stack([a[row] for a in line]).astype(jnp.int32)
    parts = pick(rnd, place, codes, line, layer, per_round)
    got = [parts[0]]
    for m in range(1, layer):
        pairs = [(z * layer + i, z * layer + (i ^ m)) for z in range(NZ) for i in range(layer)]
        got.append(lax.ppermute(parts[m], AXES, pairs))
    return got, tie


def block_order(place, wide, cols):
    chips, own = cols // 2, wide // cols
    x, core = place[2], place[3]
    return [(lax.rem(x + j, chips) * 2 + (core ^ part)) * own + o for part in range(2) for j in range(chips) for o in range(own)]


def split_kernel(per_step, wide, cols, place, source, both):
    edge = both.shape[1] // 2
    order = block_order(place, wide, cols)
    for c in range(per_step):
        for a in range(wide):
            x = source[pl.ds(c * edge * wide + order[a], edge, stride=wide), :]
            h = x.astype(bf16)
            both[c, :edge, a * edge : (a + 1) * edge] = h
            both[c, edge:, a * edge : (a + 1) * edge] = (x - h.astype(f32)).astype(bf16)


def split(place, integrals, cols):
    rows, wide, edge = integrals.shape
    blocks = rows // edge
    per_step = 4
    return pl.pallas_call(
        functools.partial(split_kernel, per_step, wide, cols),
        grid_spec=pltpu.PrefetchScalarGridSpec(
            num_scalar_prefetch=1,
            grid=(blocks // per_step,),
            in_specs=[pl.BlockSpec((per_step * edge * wide, edge), lambda i, at: (i, 0))],
            out_specs=pl.BlockSpec((per_step, 2 * edge, wide * edge), lambda i, at: (i, 0, 0)),
        ),
        out_shape=jax.ShapeDtypeStruct((blocks, 2 * edge, wide * edge), bf16),
        compiler_params=pltpu.CompilerParams(vmem_limit_bytes=16 << 20),
        cost_estimate=pl.CostEstimate(flops=0, bytes_accessed=2 * rows * wide * edge * 4, transcendentals=0),
        name="split",
    )(place, integrals.reshape(rows * wide, edge))


def product_kernel(layer, firsts, low_occ, occs, per_round, cols, own, rnd, place, table, *refs):
    sources, refs = refs[:layer][::-1], refs[layer:]
    if firsts:
        first, refs = refs[0], refs[1:]
    both, keep, give, tiles, held, queue, sem_t, sem_b = refs
    edge = both.shape[1] // 2
    wide = both.shape[2] // edge
    count = layer * NZ
    blocks = [(out, j, o) for out in (keep, give) for j in range(cols // 2) for o in range(own)]
    mine = place[1]
    dot = functools.partial(jnp.dot, preferred_element_type=f32)

    slots = held.shape[0]

    def enter(base, n, where, number, ok):
        pair = number - 1
        p = pair >> CV_BITS
        queue[3 * (base + n)] = where
        queue[3 * (base + n) + 1] = p - low_occ
        queue[3 * (base + n) + 2] = pair & (CV_DEV - 1)
        ok = ok & (number > 0) & (p >= low_occ) & (p < low_occ + occs)
        return ok, n + ok.astype(jnp.int32)

    def pad(n):
        for u in range(3 * GROUP):
            queue[3 * n + u] = 0

    def fetch(g, u):
        slot = lax.rem(g, slots)
        return pltpu.make_async_copy(both.at[queue[3 * (g * GROUP + u) + 2]], held.at[slot, u], sem_b.at[slot, u])

    def ahead(g, groups):
        @pl.when(g < groups)
        def _():
            for u in range(GROUP):
                fetch(g, u).start()

    def work(ref, low, high, base, total, groups):
        def step(g, c):
            ahead(g + slots - 1, groups)
            for u in range(GROUP):
                fetch(g, u).wait()
            for u in range(GROUP):
                n = g * GROUP + u
                a = jnp.where(n - base < total, ref[queue[3 * n]], 0.0)
                ah = a.astype(bf16)
                al = (a - ah.astype(f32)).astype(bf16)
                b = held.at[lax.rem(g, slots), u]
                r = dot(jnp.concatenate([ah, ah], axis=1), b[...]) + dot(al, b[:edge, :])
                at = pl.ds(pl.multiple_of(queue[3 * n + 1] * edge, edge), edge)
                for k, (out, j, o) in enumerate(blocks):
                    out[j, o, at, :] += r[:, k * edge : (k + 1) * edge]
            return c

        lax.fori_loop(low, high, step, 0)

    total = jnp.int32(0)
    if firsts:

        def listing(i, n):
            m, at = layer - 1 - i // NZ, i % NZ
            return enter(0, n, at * layer + (mine ^ m), table[i] & MASK, True)[1]

        total = lax.fori_loop(0, count, listing, total, unroll=4)
        pad(total)
    early = (total + GROUP - 1) // GROUP
    for g in range(slots - 1):
        ahead(jnp.int32(g), early)

    seconds = jnp.int32(0)
    for m in range(layer):
        for k in range(NZ):
            code = table[(layer - 1 - m) * NZ + k]
            here = (code >> (2 * SHIFT)) - rnd[0] * per_round
            ok, more = enter(GROUP * early, seconds, seconds, (code >> SHIFT) & MASK, (here >= 0) & (here < per_round))

            @pl.when(ok)
            def _():
                pltpu.make_async_copy(sources[m].at[pl.ds(k * edge, edge), :], tiles.at[seconds], sem_t.at[seconds]).start()

            seconds = more
    pad(GROUP * early + seconds)
    groups = early + (seconds + GROUP - 1) // GROUP
    for g in range(slots - 1):

        @pl.when(g >= early)
        def _():
            ahead(jnp.int32(g), groups)

    keep[...] = jnp.zeros_like(keep)
    give[...] = jnp.zeros_like(give)
    if firsts:
        work(first, 0, early, 0, total, groups)

    def arrive(n, c):
        pltpu.make_async_copy(sources[0].at[pl.ds(0, edge), :], tiles.at[n], sem_t.at[n]).wait()
        return c

    lax.fori_loop(0, seconds, arrive, 0)
    work(tiles, early, groups, GROUP * early, seconds, groups)


def product(rnd, place, table, second, first, both, layer, per_round, cols, own, low_occ, occs):
    edge = both.shape[1] // 2
    wide = both.shape[2] // edge
    rows = occs * edge
    chips = cols // 2
    count = layer * NZ
    firsts = first is not None
    operands = [pltpu.with_memory_space_constraint(a, pltpu.HBM) for a in reversed(second)]
    if firsts:
        operands.append(pltpu.with_memory_space_constraint(first, pltpu.VMEM))
    out = pltpu.VMEM((chips, own, rows, edge), f32)
    return pl.pallas_call(
        functools.partial(product_kernel, layer, firsts, low_occ, occs, per_round, cols, own),
        grid_spec=pltpu.PrefetchScalarGridSpec(
            num_scalar_prefetch=3,
            in_specs=[ANY] * len(second) + [pl.BlockSpec(memory_space=pltpu.VMEM)] * firsts + [ANY],
            out_specs=[pl.BlockSpec(memory_space=pltpu.VMEM)] * 2,
            scratch_shapes=[
                pltpu.VMEM((count, edge, edge), f32),
                pltpu.VMEM((SLOTS, GROUP, 2 * edge, wide * edge), bf16),
                pltpu.SMEM((6 * (count + GROUP),), jnp.int32),
                pltpu.SemaphoreType.DMA((count,)),
                pltpu.SemaphoreType.DMA((SLOTS, GROUP)),
            ],
        ),
        out_shape=[out, out],
        compiler_params=pltpu.CompilerParams(vmem_limit_bytes=room((count, edge, edge), (SLOTS * GROUP, edge, wide * edge), (wide, rows, edge), (GROUP, edge, 2 * wide * edge))),
        cost_estimate=pl.CostEstimate(flops=4 * count * edge * edge * edge * wide, bytes_accessed=16 << 20, transcendentals=0),
        name="product",
    )(rnd, place, table, *operands, both)


def chip_sum(keep, give, cols):
    got = lax.ppermute(give, "col", [(c, c ^ 1) for c in range(cols)])
    return [keep[j] + got[j] for j in range(cols // 2)]


def exchange(sums, cols):
    chips = cols // 2
    return [lax.ppermute(sums[j], "col", [(c, (c // 2 + j) % chips * 2 + c % 2) for c in range(cols)]) for j in range(1, chips)]


def body(amplitudes, amp_owner, amp_occ, amp_vir, integrals):
    rows, cols = lax.axis_size("row"), lax.axis_size("col")
    devices = rows * cols
    layer = devices // NZ
    per_round = max(1, amplitudes.shape[0] // 8)
    own = integrals.shape[1] // cols
    edge = amplitudes.shape[1]
    row, col = lax.axis_index("row"), lax.axis_index("col")
    me = row * cols + col
    place = jnp.stack([me // layer, me % layer, col // 2, col % 2]).astype(jnp.int32)
    owner = amp_owner[:, 0]

    def packed(r):
        return pack(r, owner, amp_occ, amp_vir, amplitudes, devices, per_round)

    zero = jnp.zeros((1,), jnp.int32)
    send, pay = packed(zero)
    first = lax.all_to_all(send, AXES, split_axis=0, concat_axis=0, tiled=True)
    got, both = overflow_round(zero, place, pay, layer, per_round, split(place, integrals, cols))
    heads = jnp.stack([g[NZ * edge :].reshape(NZ, HEAD, 128)[:, 0] for g in reversed(got)]).astype(jnp.int32)
    table = lax.dynamic_index_in_dim(heads, me, 2, keepdims=False).reshape(-1)
    most = jnp.max(jnp.sum(((heads >> SHIFT) & MASK) > 0, axis=2, dtype=jnp.int32))
    rounds = (most + per_round - 1) // per_round

    def run(r, table, second, firsts, low_occ, occs):
        return product(r, place, table, second, firsts, both, layer, per_round, cols, own, low_occ, occs)

    pieces, moved = [], None
    for g, occs in enumerate(SPANS):
        keep, give = run(zero, table, got, first, sum(SPANS[:g]), occs)
        if moved is not None:
            give, moved = lax.optimization_barrier((give, moved))
            pieces.append(functools.reduce(jnp.add, moved, sums[0]))
        sums = chip_sum(keep, give, cols)
        sums, table = lax.optimization_barrier((sums, table))
        moved = exchange(sums, cols)
    pieces.append(functools.reduce(jnp.add, moved, sums[0]))
    out = jnp.concatenate(pieces, axis=1)

    def more(carry):
        r, total = carry
        at = jnp.reshape(r, (1,))
        again, _ = overflow_round(at, place, packed(at)[1], layer, per_round, place)
        sums = chip_sum(*run(at, table, again, None, 0, OCC_DEV), cols)
        return r + 1, functools.reduce(jnp.add, exchange(sums, cols), total + sums[0])

    return lax.while_loop(lambda c: c[0] < rounds, more, (jnp.int32(1), out))[1]


def solution(mesh):
    in_specs = (
        P(("row", "col"), None, None),
        P(("row", "col"), None),
        P(("row", "col")),
        P(("row", "col")),
        P("col", None, None),
    )
    out_specs = P("col", "row", None)
    return jax.shard_map(body, mesh=mesh, in_specs=in_specs, out_specs=out_specs, check_vma=False)
```

```python
import functools
import math

import jax
import jax.numpy as jnp
from jax import lax
from jax.experimental import pallas as pl
from jax.experimental.pallas import tpu as pltpu
from jax.sharding import PartitionSpec as P

CAP = 2
OCC_DEV = 12
CV_DEV = 32
CV_BITS = CV_DEV.bit_length() - 1
NZ = 4
PIECES = 4
HEAD = 8
SPANS = (5, 7)
SHIFT = 9
MASK = (1 << SHIFT) - 1
GROUP = 4
SLOTS = 5
AXES = ("row", "col")
ANY = pl.BlockSpec(memory_space=pl.ANY)
f32 = jnp.float32
bf16 = jnp.bfloat16


def room(*arrays):
    return sum(4 * math.prod(a) for a in arrays) + (6 << 20)


def pack_kernel(tiles, devices, per_round, rnd, owner, occ, vir, amp, send, pay, held, count, head, sem_in, sem_a, sem_b, sem_h):
    edge = amp.shape[1]
    piece = tiles // PIECES
    loads = [pltpu.make_async_copy(amp.at[pl.ds(i * piece, piece)], held.at[pl.ds(i * piece, piece)], sem_in.at[i]) for i in range(PIECES)]
    for load in loads:
        load.start()

    def clear(d, c):
        count[d] = 0
        head[0, d] = 0.0
        return c

    lax.fori_loop(0, devices, clear, 0, unroll=8)
    base = rnd[0] * per_round

    def first(t, d):
        return pltpu.make_async_copy(held.at[t], send.at[d], sem_a.at[d])

    def second(t, j):
        return pltpu.make_async_copy(held.at[t], pay.at[pl.ds(pl.multiple_of(j * edge, edge), edge), :], sem_b.at[j])

    def place_tile(t, j):
        o = owner[t]
        n = count[o]
        count[o] = n + 1
        pair = occ[t] * CV_DEV + vir[t] + 1
        here = j - base

        @pl.when(n == 0)
        def _():
            first(t, o).start()
            head[0, o] = pair.astype(f32)

        @pl.when(n > 0)
        def _():
            head[0, o] = head[0, o] + ((pair << SHIFT) + (j << (2 * SHIFT))).astype(f32)

        @pl.when((n > 0) & (here >= 0) & (here < per_round))
        def _():
            second(t, here).start()

        return j + (n > 0).astype(jnp.int32)

    total = jnp.int32(0)
    for i in range(PIECES):
        loads[i].wait()
        total = lax.fori_loop(i * piece, (i + 1) * piece, place_tile, total, unroll=4)
    copy = pltpu.make_async_copy(head, pay.at[pl.ds(per_round * edge, HEAD), :], sem_h)
    copy.start()

    for j in range(per_round):

        @pl.when(base + j < total)
        def _():
            second(0, j).wait()

    copy.wait()

    def settle(d, c):
        @pl.when(count[d] > 0)
        def _():
            first(0, d).wait()

        return c

    lax.fori_loop(0, devices, settle, 0, unroll=8)


def pack(rnd, owner, occ, vir, amp, devices, per_round):
    tiles, edge = amp.shape[:2]
    return pl.pallas_call(
        functools.partial(pack_kernel, tiles, devices, per_round),
        grid_spec=pltpu.PrefetchScalarGridSpec(
            num_scalar_prefetch=4,
            in_specs=[ANY],
            out_specs=[pl.BlockSpec(memory_space=pltpu.HBM), pl.BlockSpec(memory_space=pltpu.VMEM)],
            scratch_shapes=[
                pltpu.VMEM((tiles, edge, edge), f32),
                pltpu.SMEM((devices,), jnp.int32),
                pltpu.SMEM((HEAD, 128), f32),
                pltpu.SemaphoreType.DMA((PIECES,)),
                pltpu.SemaphoreType.DMA((devices,)),
                pltpu.SemaphoreType.DMA((per_round,)),
                pltpu.SemaphoreType.DMA,
            ],
        ),
        out_shape=[
            pltpu.HBM((devices, edge, edge), f32),
            jax.ShapeDtypeStruct((per_round * edge + HEAD, edge), f32),
        ],
        compiler_params=pltpu.CompilerParams(vmem_limit_bytes=room(amp.shape, (per_round * edge, edge))),
        name="pack",
    )(rnd, owner, occ, vir, amp)


def pick_kernel(layer, per_round, rnd, place, codes, *refs):
    line = refs[:NZ]
    outs = refs[NZ:]
    edge = line[0].shape[1]
    z, mine = place[0], place[1]
    for k in range(NZ):
        at = z ^ k
        head = line[k][pl.ds(per_round * edge, HEAD), :]
        for m in range(layer):
            code = codes[k, z * layer + (mine ^ m)]
            here = (code >> (2 * SHIFT)) - rnd[0] * per_round
            full = ((code >> SHIFT) & MASK) > 0

            @pl.when(full & (here >= 0) & (here < per_round))
            def _():
                rows = pl.ds(pl.multiple_of(here * edge, edge), edge)
                outs[m][pl.ds(pl.multiple_of(at * edge, edge), edge), :] = line[k][rows, :]

            outs[m][pl.ds(pl.multiple_of(NZ * edge + at * HEAD, HEAD), HEAD), :] = head


def pick(rnd, place, codes, arrays, layer, per_round):
    rows, edge = arrays[0].shape
    whole = pl.BlockSpec(memory_space=pltpu.VMEM)
    return pl.pallas_call(
        functools.partial(pick_kernel, layer, per_round),
        grid_spec=pltpu.PrefetchScalarGridSpec(
            num_scalar_prefetch=3,
            in_specs=[whole] * NZ,
            out_specs=[whole] * layer,
        ),
        out_shape=[jax.ShapeDtypeStruct((NZ * (edge + HEAD), edge), f32)] * layer,
        compiler_params=pltpu.CompilerParams(vmem_limit_bytes=room((NZ, rows, edge), (layer, NZ * (edge + HEAD), edge))),
        name="pick",
    )(rnd, place, codes, *arrays)


def overflow_round(rnd, place, pay, layer, per_round, tie):
    row = per_round * pay.shape[1]

    def along(k):
        return [(z * layer + i, (z ^ k) * layer + i) for z in range(NZ) for i in range(layer)]

    cross = lax.ppermute(pay, AXES, along(2))
    near = lax.ppermute(pay, AXES, along(1))
    cross, tie = lax.optimization_barrier((cross, tie))
    line = [pay, near, cross, lax.ppermute(cross, AXES, along(1))]
    codes = jnp.stack([a[row] for a in line]).astype(jnp.int32)
    parts = pick(rnd, place, codes, line, layer, per_round)
    got = [parts[0]]
    for m in range(1, layer):
        pairs = [(z * layer + i, z * layer + (i ^ m)) for z in range(NZ) for i in range(layer)]
        got.append(lax.ppermute(parts[m], AXES, pairs))
    return got, tie


def block_order(place, wide, cols):
    chips, own = cols // 2, wide // cols
    x, core = place[2], place[3]
    return [(lax.rem(x + j, chips) * 2 + (core ^ part)) * own + o for part in range(2) for j in range(chips) for o in range(own)]


def split_kernel(per_step, wide, cols, place, source, both):
    edge = both.shape[1] // 2
    order = block_order(place, wide, cols)
    for c in range(per_step):
        for a in range(wide):
            x = source[pl.ds(c * edge * wide + order[a], edge, stride=wide), :]
            h = x.astype(bf16)
            both[c, :edge, a * edge : (a + 1) * edge] = h
            both[c, edge:, a * edge : (a + 1) * edge] = (x - h.astype(f32)).astype(bf16)


def split(place, integrals, cols):
    rows, wide, edge = integrals.shape
    blocks = rows // edge
    per_step = 4
    return pl.pallas_call(
        functools.partial(split_kernel, per_step, wide, cols),
        grid_spec=pltpu.PrefetchScalarGridSpec(
            num_scalar_prefetch=1,
            grid=(blocks // per_step,),
            in_specs=[pl.BlockSpec((per_step * edge * wide, edge), lambda i, at: (i, 0))],
            out_specs=pl.BlockSpec((per_step, 2 * edge, wide * edge), lambda i, at: (i, 0, 0)),
        ),
        out_shape=jax.ShapeDtypeStruct((blocks, 2 * edge, wide * edge), bf16),
        compiler_params=pltpu.CompilerParams(vmem_limit_bytes=16 << 20),
        cost_estimate=pl.CostEstimate(flops=0, bytes_accessed=2 * rows * wide * edge * 4, transcendentals=0),
        name="split",
    )(place, integrals.reshape(rows * wide, edge))


def product_kernel(layer, firsts, low_occ, occs, per_round, cols, own, rnd, place, table, *refs):
    sources, refs = refs[:layer][::-1], refs[layer:]
    if firsts:
        first, refs = refs[0], refs[1:]
    both, keep, give, tiles, held, queue, sem_t, sem_b = refs
    edge = both.shape[1] // 2
    wide = both.shape[2] // edge
    count = layer * NZ
    blocks = [(out, j, o) for out in (keep, give) for j in range(cols // 2) for o in range(own)]
    mine = place[1]
    dot = functools.partial(jnp.dot, preferred_element_type=f32)

    slots = held.shape[0]

    def enter(base, n, where, number, ok):
        pair = number - 1
        p = pair >> CV_BITS
        queue[3 * (base + n)] = where
        queue[3 * (base + n) + 1] = p - low_occ
        queue[3 * (base + n) + 2] = pair & (CV_DEV - 1)
        ok = ok & (number > 0) & (p >= low_occ) & (p < low_occ + occs)
        return ok, n + ok.astype(jnp.int32)

    def pad(n):
        for u in range(3 * GROUP):
            queue[3 * n + u] = 0

    def fetch(g, u):
        slot = lax.rem(g, slots)
        return pltpu.make_async_copy(both.at[queue[3 * (g * GROUP + u) + 2]], held.at[slot, u], sem_b.at[slot, u])

    def ahead(g, groups):
        @pl.when(g < groups)
        def _():
            for u in range(GROUP):
                fetch(g, u).start()

    def work(ref, low, high, base, total, groups):
        def step(g, c):
            ahead(g + slots - 1, groups)
            for u in range(GROUP):
                fetch(g, u).wait()
            for u in range(GROUP):
                n = g * GROUP + u
                a = jnp.where(n - base < total, ref[queue[3 * n]], 0.0)
                ah = a.astype(bf16)
                al = (a - ah.astype(f32)).astype(bf16)
                b = held.at[lax.rem(g, slots), u]
                r = dot(jnp.concatenate([ah, ah], axis=1), b[...]) + dot(al, b[:edge, :])
                at = pl.ds(pl.multiple_of(queue[3 * n + 1] * edge, edge), edge)
                for k, (out, j, o) in enumerate(blocks):
                    out[j, o, at, :] += r[:, k * edge : (k + 1) * edge]
            return c

        lax.fori_loop(low, high, step, 0)

    total = jnp.int32(0)
    if firsts:

        def listing(i, n):
            m, at = layer - 1 - i // NZ, i % NZ
            return enter(0, n, at * layer + (mine ^ m), table[i] & MASK, True)[1]

        total = lax.fori_loop(0, count, listing, total, unroll=4)
        pad(total)
    early = (total + GROUP - 1) // GROUP
    for g in range(slots - 1):
        ahead(jnp.int32(g), early)

    seconds = jnp.int32(0)
    for m in range(layer):
        for k in range(NZ):
            code = table[(layer - 1 - m) * NZ + k]
            here = (code >> (2 * SHIFT)) - rnd[0] * per_round
            ok, more = enter(GROUP * early, seconds, seconds, (code >> SHIFT) & MASK, (here >= 0) & (here < per_round))

            @pl.when(ok)
            def _():
                pltpu.make_async_copy(sources[m].at[pl.ds(k * edge, edge), :], tiles.at[seconds], sem_t.at[seconds]).start()

            seconds = more
    pad(GROUP * early + seconds)
    groups = early + (seconds + GROUP - 1) // GROUP
    for g in range(slots - 1):

        @pl.when(g >= early)
        def _():
            ahead(jnp.int32(g), groups)

    keep[...] = jnp.zeros_like(keep)
    give[...] = jnp.zeros_like(give)
    if firsts:
        work(first, 0, early, 0, total, groups)

    def arrive(n, c):
        pltpu.make_async_copy(sources[0].at[pl.ds(0, edge), :], tiles.at[n], sem_t.at[n]).wait()
        return c

    lax.fori_loop(0, seconds, arrive, 0)
    work(tiles, early, groups, GROUP * early, seconds, groups)


def product(rnd, place, table, second, first, both, layer, per_round, cols, own, low_occ, occs):
    edge = both.shape[1] // 2
    wide = both.shape[2] // edge
    rows = occs * edge
    chips = cols // 2
    count = layer * NZ
    firsts = first is not None
    operands = [pltpu.with_memory_space_constraint(a, pltpu.HBM) for a in reversed(second)]
    if firsts:
        operands.append(pltpu.with_memory_space_constraint(first, pltpu.VMEM))
    out = pltpu.VMEM((chips, own, rows, edge), f32)
    return pl.pallas_call(
        functools.partial(product_kernel, layer, firsts, low_occ, occs, per_round, cols, own),
        grid_spec=pltpu.PrefetchScalarGridSpec(
            num_scalar_prefetch=3,
            in_specs=[ANY] * len(second) + [pl.BlockSpec(memory_space=pltpu.VMEM)] * firsts + [ANY],
            out_specs=[pl.BlockSpec(memory_space=pltpu.VMEM)] * 2,
            scratch_shapes=[
                pltpu.VMEM((count, edge, edge), f32),
                pltpu.VMEM((SLOTS, GROUP, 2 * edge, wide * edge), bf16),
                pltpu.SMEM((6 * (count + GROUP),), jnp.int32),
                pltpu.SemaphoreType.DMA((count,)),
                pltpu.SemaphoreType.DMA((SLOTS, GROUP)),
            ],
        ),
        out_shape=[out, out],
        compiler_params=pltpu.CompilerParams(vmem_limit_bytes=room((count, edge, edge), (SLOTS * GROUP, edge, wide * edge), (wide, rows, edge), (GROUP, edge, 2 * wide * edge))),
        cost_estimate=pl.CostEstimate(flops=4 * count * edge * edge * edge * wide, bytes_accessed=16 << 20, transcendentals=0),
        name="product",
    )(rnd, place, table, *operands, both)


def chip_sum(keep, give, cols):
    got = lax.ppermute(give, "col", [(c, c ^ 1) for c in range(cols)])
    return [keep[j] + got[j] for j in range(cols // 2)]


def exchange(sums, cols):
    chips = cols // 2
    return [lax.ppermute(sums[j], "col", [(c, (c // 2 + j) % chips * 2 + c % 2) for c in range(cols)]) for j in range(1, chips)]


def body(amplitudes, amp_owner, amp_occ, amp_vir, integrals):
    rows, cols = lax.axis_size("row"), lax.axis_size("col")
    devices = rows * cols
    layer = devices // NZ
    per_round = max(1, amplitudes.shape[0] // 8)
    own = integrals.shape[1] // cols
    edge = amplitudes.shape[1]
    row, col = lax.axis_index("row"), lax.axis_index("col")
    me = row * cols + col
    place = jnp.stack([me // layer, me % layer, col // 2, col % 2]).astype(jnp.int32)
    owner = amp_owner[:, 0]

    def packed(r):
        return pack(r, owner, amp_occ, amp_vir, amplitudes, devices, per_round)

    zero = jnp.zeros((1,), jnp.int32)
    send, pay = packed(zero)
    first = lax.all_to_all(send, AXES, split_axis=0, concat_axis=0, tiled=True)
    got, both = overflow_round(zero, place, pay, layer, per_round, split(place, integrals, cols))
    heads = jnp.stack([g[NZ * edge :].reshape(NZ, HEAD, 128)[:, 0] for g in reversed(got)]).astype(jnp.int32)
    table = lax.dynamic_index_in_dim(heads, me, 2, keepdims=False).reshape(-1)
    most = jnp.max(jnp.sum(((heads >> SHIFT) & MASK) > 0, axis=2, dtype=jnp.int32))
    rounds = (most + per_round - 1) // per_round

    def run(r, table, second, firsts, low_occ, occs):
        return product(r, place, table, second, firsts, both, layer, per_round, cols, own, low_occ, occs)

    pieces, moved = [], None
    for g, occs in enumerate(SPANS):
        keep, give = run(zero, table, got, first, sum(SPANS[:g]), occs)
        if moved is not None:
            give, moved = lax.optimization_barrier((give, moved))
            pieces.append(functools.reduce(jnp.add, moved, sums[0]))
        sums = chip_sum(keep, give, cols)
        sums, table = lax.optimization_barrier((sums, table))
        moved = exchange(sums, cols)
    pieces.append(functools.reduce(jnp.add, moved, sums[0]))
    out = jnp.concatenate(pieces, axis=1)

    def more(carry):
        r, total = carry
        at = jnp.reshape(r, (1,))
        again, _ = overflow_round(at, place, packed(at)[1], layer, per_round, place)
        sums = chip_sum(*run(at, table, again, None, 0, OCC_DEV), cols)
        return r + 1, functools.reduce(jnp.add, exchange(sums, cols), total + sums[0])

    return lax.while_loop(lambda c: c[0] < rounds, more, (jnp.int32(1), out))[1]


def solution(mesh):
    in_specs = (
        P(("row", "col"), None, None),
        P(("row", "col"), None),
        P(("row", "col")),
        P(("row", "col")),
        P("col", None, None),
    )
    out_specs = P("col", "row", None)
    return jax.shard_map(body, mesh=mesh, in_specs=in_specs, out_specs=out_specs, check_vma=False)
```
